128 devices in a mesh: node: 16 (over y, x), local: 8 (over z, core).
Axes of the slice: x: 4, y: 4, z: 4, core: 2. Of those that a mesh axis runs over, the one named last changes fastest.
Arguments:
- tokens: bfloat16 [2048, 4096], P(('node', 'local')), may hold values from -6 to 6
- expert_ids: int32 [2048, 8], P(('node', 'local')), may hold values from 0 to 127, all different within a row; in each aligned block of 16 rows (0 to 15, 16 to 31, ...) at most 2 rows name the same one
- combine: float32 [2048, 8], P(('node', 'local')), may hold values from 0.1 to 1
- w_gate: bfloat16 [128, 4096, 768], P(('node', 'local')), may hold values from -0.09375 to 0.09375
- w_up: bfloat16 [128, 4096, 768], P(('node', 'local')), may hold values from -0.09375 to 0.09375
- w_down: bfloat16 [128, 768, 4096], P(('node', 'local')), may hold values from -0.21875 to 0.21875
- grad_out: bfloat16 [2048, 4096], P(('node', 'local')), may hold values from -6 to 6
Outputs:
- mixed: bfloat16 [2048, 4096], P(('node', 'local'))
- input_grad: bfloat16 [2048, 4096], P(('node', 'local'))
- combine_grad: float32 [2048, 8], P(('node', 'local'))
The draws below stay inside these ranges and needn't reach their ends.
Inputs may be any that keep to these rules, and one draw needn't show every extreme that they name: `expert_ids`: each token names 8 different experts. Among the tokens of one device (aligned blocks of 16 tokens) no expert is named by more than 2 of them, a bound that some block reaches.
All inputs are finite; a program needn't handle non-finite values.
Results may differ from the reference program's by a relative error of at most 0.0065.
Values may be sent and summed in bfloat16 or wider, within the bound.
A program may use at most 128 MiB of HBM per device.

```python
import math
import jax
import jax.numpy as jnp
import numpy as np
from jax import lax

D = 4096
HID = 768
TOP = 8
TOK_DEV = 16
EXPERTS = 128
CAP = 2
TOKENS = 2048
DEVICES = 128


def block_scale(own_key, shape, cuts, smallest, largest):
    def one(position, parts):
        steps = jax.random.uniform(jax.random.fold_in(jax.random.fold_in(own_key, 6), position), (parts,), jnp.float32, smallest / len(cuts), largest / len(cuts))
        return jnp.repeat(jnp.exp(steps), shape[position] // parts).reshape((-1,) + (1,) * (len(shape) - position - 1))

    loudness = one(*cuts[0])
    for cut in cuts[1:]:
        loudness = loudness * one(*cut)
    return loudness


def deal_out(stream_key, own, number, rows, count, top, most, lean):
    sequence = jax.random.permutation(stream_key, count)
    heavy_load, common = shares(count, rows * top, most, lean, True), shares(count, rows * top, most, lean, False)
    places = jnp.arange(count)

    def named(lengths, offset_by):
        used = int((lengths > 0).sum())
        fixed = max(1, used // 4)
        passed = fixed + (places - fixed + offset_by * (used - fixed)) % max(1, count - fixed)
        return jnp.zeros((count,), jnp.int32).at[sequence[jnp.where(places < fixed, places, passed)]].set(jnp.asarray(lengths, jnp.int32))

    lengths = jnp.where(number % 4 == 0, named(heavy_load, number // 4), named(common, number - number // 4 - 1))
    mixed = jax.random.permutation(jax.random.fold_in(own, 3), count)
    donor, sink = mixed[0:count // 2 * 2:2], mixed[1:count // 2 * 2:2]
    room = jnp.minimum(lengths[donor] - 1, most - lengths[sink]) // 2
    room = jnp.where((donor == sequence[0]) | (sink == sequence[0]) | (lengths[sink] == 0), 0, jnp.maximum(room, 0))
    passed = jax.random.randint(jax.random.fold_in(own, 4), (count // 2,), 0, 1 << 20) % (room + 1)
    lengths = lengths.at[donor].add(-passed).at[sink].add(passed)
    items = jnp.searchsorted(jnp.cumsum(lengths), jnp.arange(rows * top), side="right").astype(jnp.int32)
    table = items.reshape(top, rows).T
    table = table[jax.random.permutation(jax.random.fold_in(own, 1), rows)]
    offset_by = jax.random.randint(jax.random.fold_in(own, 2), (rows, 1), 0, top)
    return jnp.take_along_axis(table, (jnp.arange(top)[None, :] + offset_by) % top, axis=1)


def shares(number_of, total, limit, lean, full):
    portions = [(1 << 20) // math.isqrt(grade ** lean) + 1 for grade in range(1, number_of + 1)]
    largest = limit if full else min(limit, max(-(-total // number_of), total * portions[0] // sum(portions)))
    least = 1 if total - largest >= number_of - 1 else 0
    given, surplus = [largest] + [least] * (number_of - 1), total - largest - least * (number_of - 1)
    while surplus > 0:
        candidates = [i for i in range(1, number_of) if given[i] < largest] or [i for i in range(1, number_of) if given[i] < limit]
        mass, remaining = sum([portions[i] for i in candidates]), surplus
        for i in candidates:
            addition = min(limit - given[i], max(1, remaining * portions[i] // mass), surplus)
            given[i] = given[i] + addition
            surplus = surplus - addition
    return np.array(given)


def normal_values(rng, extent, scale, limit, pieces=(), kind=jnp.bfloat16):
    level = block_scale(rng, extent, pieces, -0.22, 0.18) if pieces else 1.0
    result = jax.random.normal(rng, extent, jnp.float32) * scale * level
    return jnp.minimum(jnp.maximum(result, -limit), limit).astype(kind)


def setup_inputs(seed: int = 0) -> dict:
    arg_keys = jax.random.split(jax.random.key(seed), 8)
    tokens = normal_values(arg_keys[0], (TOKENS, D), 1.0, 6.0, ((0, 128),))
    expert_ids_keys = jax.random.split(jax.random.fold_in(arg_keys[1], 1), TOKENS // TOK_DEV)
    expert_ids_turns = jax.random.permutation(jax.random.fold_in(arg_keys[1], 3), TOKENS // TOK_DEV)
    expert_ids = jax.vmap(lambda own, number: deal_out(jax.random.fold_in(arg_keys[1], 2), own, number, TOK_DEV, EXPERTS, TOP, CAP, 2))(expert_ids_keys, expert_ids_turns).reshape((TOKENS, TOP))
    combine = jnp.clip(0.1 + 0.9 * jax.random.uniform(arg_keys[2], (TOKENS, TOP), jnp.float32) ** block_scale(arg_keys[2], (TOKENS, TOP), ((0, 128),), -0.2, 0.2), 0.1, 1.0)
    w_gate = normal_values(arg_keys[3], (EXPERTS, D, HID), D ** -0.5, 0.09375, ((0, 128),))
    w_up = normal_values(arg_keys[4], (EXPERTS, D, HID), D ** -0.5, 0.09375, ((0, 128),))
    w_down = normal_values(arg_keys[5], (EXPERTS, HID, D), HID ** -0.5, 0.21875, ((0, 128),))
    grad_out = normal_values(arg_keys[6], (TOKENS, D), 1.0, 6.0, ((0, 128),))
    return dict(tokens=tokens, expert_ids=expert_ids, combine=combine, w_gate=w_gate, w_up=w_up, w_down=w_down, grad_out=grad_out)


def reference(tokens, expert_ids, combine, w_gate, w_up, w_down, grad_out):
    per_dev = TOK_DEV * TOP
    ids = expert_ids.reshape(DEVICES, per_dev).astype(jnp.int32)
    onehot = (ids[:, :, None] == jnp.arange(EXPERTS, dtype=jnp.int32)[None, None, :]).astype(jnp.int32)
    earlier = jnp.cumsum(onehot, axis=1) - onehot
    slot = jnp.sum(earlier * onehot, axis=2).astype(jnp.int32)
    source = jnp.arange(DEVICES, dtype=jnp.int32)[:, None]
    target = ((ids * DEVICES + source) * CAP + slot).reshape(-1).astype(jnp.int32)
    pair_token = (jnp.arange(TOKENS * TOP, dtype=jnp.int32) // TOP).astype(jnp.int32)
    table = jnp.full((EXPERTS * DEVICES * CAP,), TOKENS, dtype=jnp.int32).at[target].set(pair_token)
    weight_table = jnp.zeros((EXPERTS * DEVICES * CAP,), jnp.float32).at[target].set(combine.reshape(-1))
    zero_row = jnp.zeros((1, D), tokens.dtype)
    token_pad = jnp.concatenate([tokens, zero_row], axis=0)
    grad_pad = jnp.concatenate([grad_out, zero_row.astype(grad_out.dtype)], axis=0)

    def per_expert(carry, inputs):
        mixed_acc, input_acc = carry
        wg, wu, wd, index, weight = inputs
        rows = token_pad[index]
        grads_in = grad_pad[index]
        gate = jnp.dot(rows, wg, preferred_element_type=jnp.float32)
        upper = jnp.dot(rows, wu, preferred_element_type=jnp.float32)
        sigma = jax.nn.sigmoid(gate)
        active = gate * sigma
        hidden = (active * upper).astype(jnp.bfloat16)
        expert_out = jnp.dot(hidden, wd, preferred_element_type=jnp.float32).astype(jnp.bfloat16)
        out_f = expert_out.astype(jnp.float32)
        mixed_acc = mixed_acc.at[index].add(weight[:, None] * out_f)
        row_dw = jnp.sum(grads_in.astype(jnp.float32) * out_f, axis=1)
        out_grad = (grads_in.astype(jnp.float32) * weight[:, None]).astype(jnp.bfloat16)
        hidden_grad = lax.dot_general(out_grad, wd, (((1,), (1,)), ((), ())), preferred_element_type=jnp.float32)
        gate_grad = (hidden_grad * upper * sigma * (1.0 + gate * (1.0 - sigma))).astype(jnp.bfloat16)
        up_grad = (hidden_grad * active).astype(jnp.bfloat16)
        row_grad = lax.dot_general(gate_grad, wg, (((1,), (1,)), ((), ())), preferred_element_type=jnp.float32)
        row_grad = row_grad + lax.dot_general(up_grad, wu, (((1,), (1,)), ((), ())), preferred_element_type=jnp.float32)
        row_grad = row_grad.astype(jnp.bfloat16)
        input_acc = input_acc.at[index].add(row_grad.astype(jnp.float32))
        return (mixed_acc, input_acc), row_dw

    start = (jnp.zeros((TOKENS + 1, D), jnp.float32), jnp.zeros((TOKENS + 1, D), jnp.float32))
    inputs = (w_gate, w_up, w_down, table.reshape(EXPERTS, DEVICES * CAP), weight_table.reshape(EXPERTS, DEVICES * CAP))
    (mixed_acc, input_acc), row_dws = lax.scan(per_expert, start, inputs)
    combine_grad = row_dws.reshape(-1)[target].reshape(TOKENS, TOP)
    mixed = mixed_acc[:TOKENS].astype(jnp.bfloat16)
    input_grad = input_acc[:TOKENS].astype(jnp.bfloat16)
    return mixed, input_grad, combine_grad
```

```python
import jax
import jax.numpy as jnp
from jax import lax
from jax.sharding import PartitionSpec as P


def to_experts(buffers, experts, cap_rows):
    width = buffers[0].shape[1]
    shaped = tuple((item.reshape(experts, cap_rows, width) for item in buffers))
    arrived = (
        lax.all_to_all(shaped[0], ("node", "local"), split_axis=0, concat_axis=0, tiled=True),
        lax.all_to_all(shaped[1], ("node", "local"), split_axis=0, concat_axis=0, tiled=True),
    )
    return tuple((item.reshape(experts * cap_rows, width) for item in arrived))


def to_tokens(buffer, experts, cap_rows):
    width = buffer.shape[1]
    shaped = buffer.reshape(experts, cap_rows, width)
    return lax.all_to_all(shaped, ("node", "local"), split_axis=0, concat_axis=0, tiled=True)


def shards(tokens, expert_ids, combine, w_gate, w_up, w_down, grad_out):
    tok_count = tokens.shape[0]
    top_count = expert_ids.shape[1]
    width = tokens.shape[1]
    experts = lax.axis_size("node") * lax.axis_size("local")
    cap_rows = max(2, 3 * tok_count * top_count // (2 * experts))
    pair_ids = expert_ids.reshape(-1)
    onehot = (pair_ids[:, None] == jnp.arange(experts, dtype=jnp.int32)[None, :]).astype(jnp.int32)
    earlier = jnp.cumsum(onehot, axis=0) - onehot
    slot = jnp.sum(earlier * onehot, axis=1)
    weights = combine.reshape(-1)
    rows = jnp.repeat(tokens, top_count, axis=0)
    grads_rep = jnp.repeat(grad_out, top_count, axis=0)
    out_grad = (grads_rep.astype(jnp.float32) * weights[:, None]).astype(jnp.bfloat16)
    target = pair_ids * cap_rows + slot
    send_rows = jnp.zeros((experts * cap_rows, width), jnp.bfloat16).at[target].set(rows)
    send_grads = jnp.zeros((experts * cap_rows, width), jnp.bfloat16).at[target].set(out_grad)
    wg = w_gate[0]
    wu = w_up[0]
    wd = w_down[0]
    arrived, grads_in = to_experts((send_rows, send_grads), experts, cap_rows)
    gate = jnp.dot(arrived, wg, preferred_element_type=jnp.float32)
    upper = jnp.dot(arrived, wu, preferred_element_type=jnp.float32)
    sigma = jax.nn.sigmoid(gate)
    active = gate * sigma
    hidden = (active * upper).astype(jnp.bfloat16)
    expert_out = jnp.dot(hidden, wd, preferred_element_type=jnp.float32).astype(jnp.bfloat16)
    returned = to_tokens(expert_out, experts, cap_rows)[pair_ids, slot].astype(jnp.float32)
    mixed = jnp.sum(
        (returned * weights[:, None]).reshape(tok_count, top_count, width), axis=1
    ).astype(jnp.bfloat16)
    combine_grad = jnp.sum(grads_rep.astype(jnp.float32) * returned, axis=1).reshape(
        tok_count, top_count
    )
    hidden_grad = lax.dot_general(
        grads_in, wd, (((1,), (1,)), ((), ())), preferred_element_type=jnp.float32
    )
    gate_grad = (hidden_grad * upper * sigma * (1.0 + gate * (1.0 - sigma))).astype(jnp.bfloat16)
    up_grad = (hidden_grad * active).astype(jnp.bfloat16)
    row_grad = lax.dot_general(
        gate_grad, wg, (((1,), (1,)), ((), ())), preferred_element_type=jnp.float32
    )
    row_grad = row_grad + lax.dot_general(
        up_grad, wu, (((1,), (1,)), ((), ())), preferred_element_type=jnp.float32
    )
    row_grad = row_grad.astype(jnp.bfloat16)
    grads_back = to_tokens(row_grad, experts, cap_rows)[pair_ids, slot].astype(jnp.float32)
    input_grad = jnp.sum(grads_back.reshape(tok_count, top_count, width), axis=1).astype(
        jnp.bfloat16
    )
    return (mixed, input_grad, combine_grad)


def solution(mesh):
    in_specs = (
        P(("node", "local"), None),
        P(("node", "local"), None),
        P(("node", "local"), None),
        P(("node", "local"), None, None),
        P(("node", "local"), None, None),
        P(("node", "local"), None, None),
        P(("node", "local"), None),
    )
    out_specs = (P(("node", "local"), None), P(("node", "local"), None), P(("node", "local"), None))
    return jax.shard_map(shards, mesh=mesh, in_specs=in_specs, out_specs=out_specs, check_vma=False)
```

```python
import jax
import jax.numpy as jnp
from jax import lax
from jax.sharding import PartitionSpec as P


def to_experts(buffers, experts, cap_rows):
    width = buffers[0].shape[2]
    shaped = buffers
    arrived = (
        lax.all_to_all(shaped[0], ("node", "local"), split_axis=0, concat_axis=0, tiled=True),
        lax.all_to_all(shaped[1], ("node", "local"), split_axis=0, concat_axis=0, tiled=True),
    )
    return tuple((item.reshape(experts * cap_rows, width) for item in arrived))


def to_tokens(buffer, experts, cap_rows):
    width = buffer.shape[1]
    shaped = buffer.reshape(experts, cap_rows, width)
    return lax.all_to_all(shaped, ("node", "local"), split_axis=0, concat_axis=0, tiled=True)


def shards(tokens, expert_ids, combine, w_gate, w_up, w_down, grad_out):
    tok_count = tokens.shape[0]
    top_count = expert_ids.shape[1]
    width = tokens.shape[1]
    experts = lax.axis_size("node") * lax.axis_size("local")
    cap_rows = max(2, 3 * tok_count * top_count // (2 * experts))
    pair_ids = expert_ids.reshape(-1)
    onehot = (pair_ids[:, None] == jnp.arange(experts, dtype=jnp.int32)[None, :]).astype(jnp.int32)
    earlier = jnp.cumsum(onehot, axis=0) - onehot
    slot = jnp.sum(earlier * onehot, axis=1)
    weights = combine.reshape(-1)
    grads_rep = jnp.repeat(grad_out, top_count, axis=0)
    target = pair_ids * cap_rows + slot
    match = target[None, :] == jnp.arange(experts * cap_rows, dtype=jnp.int32)[:, None]
    pair_token = jnp.arange(tok_count * top_count, dtype=jnp.int32) // top_count
    filled = jnp.any(match, axis=1)
    source = jnp.where(filled, jnp.sum(jnp.where(match, pair_token[None, :], 0), axis=1), tok_count)
    slot_weight = jnp.sum(jnp.where(match, weights[None, :], 0.0), axis=1)
    token_pad = jnp.concatenate([tokens, jnp.zeros((1, width), tokens.dtype)], axis=0)
    grad_pad = jnp.concatenate([grad_out, jnp.zeros((1, width), grad_out.dtype)], axis=0)
    send_rows = token_pad[source].reshape(experts, cap_rows, width)
    send_grads = (grad_pad[source].astype(jnp.float32) * slot_weight[:, None]).astype(jnp.bfloat16)
    send_grads = send_grads.reshape(experts, cap_rows, width)
    wg = w_gate[0]
    wu = w_up[0]
    wd = w_down[0]
    arrived, grads_in = to_experts((send_rows, send_grads), experts, cap_rows)
    gate = jnp.dot(arrived, wg, preferred_element_type=jnp.float32)
    upper = jnp.dot(arrived, wu, preferred_element_type=jnp.float32)
    sigma = jax.nn.sigmoid(gate)
    active = gate * sigma
    hidden = (active * upper).astype(jnp.bfloat16)
    expert_out = jnp.dot(hidden, wd, preferred_element_type=jnp.float32).astype(jnp.bfloat16)
    returned = to_tokens(expert_out, experts, cap_rows)[pair_ids, slot].astype(jnp.float32)
    mixed = jnp.sum(
        (returned * weights[:, None]).reshape(tok_count, top_count, width), axis=1
    ).astype(jnp.bfloat16)
    combine_grad = jnp.sum(grads_rep.astype(jnp.float32) * returned, axis=1).reshape(
        tok_count, top_count
    )
    hidden_grad = lax.dot_general(
        grads_in, wd, (((1,), (1,)), ((), ())), preferred_element_type=jnp.float32
    )
    gate_grad = (hidden_grad * upper * sigma * (1.0 + gate * (1.0 - sigma))).astype(jnp.bfloat16)
    up_grad = (hidden_grad * active).astype(jnp.bfloat16)
    row_grad = lax.dot_general(
        gate_grad, wg, (((1,), (1,)), ((), ())), preferred_element_type=jnp.float32
    )
    row_grad = row_grad + lax.dot_general(
        up_grad, wu, (((1,), (1,)), ((), ())), preferred_element_type=jnp.float32
    )
    row_grad = row_grad.astype(jnp.bfloat16)
    grads_back = to_tokens(row_grad, experts, cap_rows)[pair_ids, slot].astype(jnp.float32)
    input_grad = jnp.sum(grads_back.reshape(tok_count, top_count, width), axis=1).astype(
        jnp.bfloat16
    )
    return (mixed, input_grad, combine_grad)


def solution(mesh):
    in_specs = (
        P(("node", "local"), None),
        P(("node", "local"), None),
        P(("node", "local"), None),
        P(("node", "local"), None, None),
        P(("node", "local"), None, None),
        P(("node", "local"), None, None),
        P(("node", "local"), None),
    )
    out_specs = (P(("node", "local"), None), P(("node", "local"), None), P(("node", "local"), None))
    return jax.shard_map(shards, mesh=mesh, in_specs=in_specs, out_specs=out_specs, check_vma=False)
```

```python
import jax
import jax.numpy as jnp
from jax import lax
from jax.sharding import PartitionSpec as P


def to_experts(buffers, experts, cap_rows):
    width = buffers[0].shape[1]
    shaped = tuple((item.reshape(experts, cap_rows, width) for item in buffers))
    arrived = (
        lax.all_to_all(shaped[0], ("node", "local"), split_axis=0, concat_axis=0, tiled=True),
        lax.all_to_all(shaped[1], ("node", "local"), split_axis=0, concat_axis=0, tiled=True),
    )
    return tuple((item.reshape(experts * cap_rows, width) for item in arrived))


def to_tokens(buffer, experts, cap_rows):
    width = buffer.shape[1]
    shaped = buffer.reshape(experts, cap_rows, width)
    return lax.all_to_all(shaped, ("node", "local"), split_axis=0, concat_axis=0, tiled=True)


def shards(tokens, expert_ids, combine, w_gate, w_up, w_down, grad_out):
    tok_count = tokens.shape[0]
    top_count = expert_ids.shape[1]
    width = tokens.shape[1]
    experts = lax.axis_size("node") * lax.axis_size("local")
    cap_rows = max(2, 3 * tok_count * top_count // (2 * experts))
    pair_ids = expert_ids.reshape(-1)
    onehot = (pair_ids[:, None] == jnp.arange(experts, dtype=jnp.int32)[None, :]).astype(jnp.int32)
    earlier = jnp.cumsum(onehot, axis=0) - onehot
    slot = jnp.sum(earlier * onehot, axis=1)
    weights = combine.reshape(-1)
    grads_rep = jnp.repeat(grad_out, top_count, axis=0)
    target = pair_ids * cap_rows + slot
    match = target[None, :] == jnp.arange(experts * cap_rows, dtype=jnp.int32)[:, None]
    slot_token = jnp.any(match.reshape(experts * cap_rows, tok_count, top_count), axis=2)
    slot_weight = jnp.sum(jnp.where(match, weights[None, :], 0.0), axis=1)
    picker = slot_token.astype(jnp.bfloat16)
    send_rows = jnp.dot(picker, tokens, preferred_element_type=jnp.float32).astype(jnp.bfloat16)
    picked_grads = jnp.dot(picker, grad_out, preferred_element_type=jnp.float32)
    send_grads = (picked_grads * slot_weight[:, None]).astype(jnp.bfloat16)
    wg = w_gate[0]
    wu = w_up[0]
    wd = w_down[0]
    arrived, grads_in = to_experts((send_rows, send_grads), experts, cap_rows)
    gate = jnp.dot(arrived, wg, preferred_element_type=jnp.float32)
    upper = jnp.dot(arrived, wu, preferred_element_type=jnp.float32)
    sigma = jax.nn.sigmoid(gate)
    active = gate * sigma
    hidden = (active * upper).astype(jnp.bfloat16)
    expert_out = jnp.dot(hidden, wd, preferred_element_type=jnp.float32).astype(jnp.bfloat16)
    returned_all = to_tokens(expert_out, experts, cap_rows)
    hidden_grad = lax.dot_general(
        grads_in, wd, (((1,), (1,)), ((), ())), preferred_element_type=jnp.float32
    )
    gate_grad = (hidden_grad * upper * sigma * (1.0 + gate * (1.0 - sigma))).astype(jnp.bfloat16)
    up_grad = (hidden_grad * active).astype(jnp.bfloat16)
    row_grad = lax.dot_general(
        gate_grad, wg, (((1,), (1,)), ((), ())), preferred_element_type=jnp.float32
    )
    row_grad = row_grad + lax.dot_general(
        up_grad, wu, (((1,), (1,)), ((), ())), preferred_element_type=jnp.float32
    )
    row_grad = row_grad.astype(jnp.bfloat16)
    row_grad = row_grad.reshape(experts, cap_rows, width)
    returned_all, row_grad = lax.optimization_barrier((returned_all, row_grad))
    returned = returned_all[pair_ids, slot].astype(jnp.float32)
    mixed = jnp.sum(
        (returned * weights[:, None]).reshape(tok_count, top_count, width), axis=1
    ).astype(jnp.bfloat16)
    combine_grad = jnp.sum(grads_rep.astype(jnp.float32) * returned, axis=1).reshape(
        tok_count, top_count
    )
    grads_back = lax.all_to_all(row_grad, ("node", "local"), split_axis=0, concat_axis=0, tiled=True)
    input_grad = lax.dot_general(
        picker.reshape(experts, cap_rows, tok_count),
        grads_back,
        (((0, 1), (0, 1)), ((), ())),
        preferred_element_type=jnp.float32,
    ).astype(jnp.bfloat16)
    return (mixed, input_grad, combine_grad)


def solution(mesh):
    in_specs = (
        P(("node", "local"), None),
        P(("node", "local"), None),
        P(("node", "local"), None),
        P(("node", "local"), None, None),
        P(("node", "local"), None, None),
        P(("node", "local"), None, None),
        P(("node", "local"), None),
    )
    out_specs = (P(("node", "local"), None), P(("node", "local"), None), P(("node", "local"), None))
    return jax.shard_map(shards, mesh=mesh, in_specs=in_specs, out_specs=out_specs, check_vma=False)
```

```python
import jax
import jax.numpy as jnp
from jax import lax
from jax.sharding import PartitionSpec as P


def to_experts(buffers, experts, cap_rows):
    width = buffers[0].shape[1]
    shaped = tuple((item.reshape(experts, cap_rows, width) for item in buffers))
    arrived = (
        lax.all_to_all(shaped[0], ("node", "local"), split_axis=0, concat_axis=0, tiled=True),
        lax.all_to_all(shaped[1], ("node", "local"), split_axis=0, concat_axis=0, tiled=True),
    )
    return tuple((item.reshape(experts * cap_rows, width) for item in arrived))


def to_tokens(buffer, experts, cap_rows):
    width = buffer.shape[1]
    shaped = buffer.reshape(experts, cap_rows, width)
    return lax.all_to_all(shaped, ("node", "local"), split_axis=0, concat_axis=0, tiled=True)


def shards(tokens, expert_ids, combine, w_gate, w_up, w_down, grad_out):
    tok_count = tokens.shape[0]
    top_count = expert_ids.shape[1]
    width = tokens.shape[1]
    experts = lax.axis_size("node") * lax.axis_size("local")
    cap_rows = max(2, 3 * tok_count * top_count // (2 * experts))
    pair_ids = expert_ids.reshape(-1)
    named = expert_ids[:, :, None] == jnp.arange(experts, dtype=jnp.int32)[None, None, :]
    present = jnp.any(named, axis=1)
    token_weight = jnp.sum(jnp.where(named, combine[:, :, None], 0.0), axis=1)
    before = jnp.cumsum(present.astype(jnp.int32), axis=0) - present.astype(jnp.int32)
    slot = jnp.take_along_axis(before, expert_ids, axis=1).reshape(-1)
    weights = combine.reshape(-1)
    grads_rep = jnp.repeat(grad_out, top_count, axis=0)
    chosen = present[:, :, None] & (before[:, :, None] == jnp.arange(cap_rows, dtype=jnp.int32))
    slot_weight = jnp.sum(jnp.where(chosen, token_weight[:, :, None], 0.0), axis=0).reshape(-1)
    picker = jnp.transpose(chosen, (1, 2, 0)).reshape(experts * cap_rows, tok_count)
    picker = picker.astype(jnp.bfloat16)
    send_rows = jnp.dot(picker, tokens, preferred_element_type=jnp.float32).astype(jnp.bfloat16)
    picked_grads = jnp.dot(picker, grad_out, preferred_element_type=jnp.float32)
    send_grads = (picked_grads * slot_weight[:, None]).astype(jnp.bfloat16)
    wg = w_gate[0]
    wu = w_up[0]
    wd = w_down[0]
    arrived, grads_in = to_experts((send_rows, send_grads), experts, cap_rows)
    gate = jnp.dot(arrived, wg, preferred_element_type=jnp.float32)
    upper = jnp.dot(arrived, wu, preferred_element_type=jnp.float32)
    sigma = jax.nn.sigmoid(gate)
    active = gate * sigma
    hidden = (active * upper).astype(jnp.bfloat16)
    expert_out = jnp.dot(hidden, wd, preferred_element_type=jnp.float32).astype(jnp.bfloat16)
    returned_all = to_tokens(expert_out, experts, cap_rows)
    hidden_grad = lax.dot_general(
        grads_in, wd, (((1,), (1,)), ((), ())), preferred_element_type=jnp.float32
    )
    gate_grad = (hidden_grad * upper * sigma * (1.0 + gate * (1.0 - sigma))).astype(jnp.bfloat16)
    up_grad = (hidden_grad * active).astype(jnp.bfloat16)
    row_grad = lax.dot_general(
        gate_grad, wg, (((1,), (1,)), ((), ())), preferred_element_type=jnp.float32
    )
    row_grad = row_grad + lax.dot_general(
        up_grad, wu, (((1,), (1,)), ((), ())), preferred_element_type=jnp.float32
    )
    row_grad = row_grad.astype(jnp.bfloat16)
    row_grad = row_grad.reshape(experts, cap_rows, width)
    returned_all, row_grad = lax.optimization_barrier((returned_all, row_grad))
    returned = returned_all[pair_ids, slot].astype(jnp.float32)
    mixed = jnp.sum(
        (returned * weights[:, None]).reshape(tok_count, top_count, width), axis=1
    ).astype(jnp.bfloat16)
    combine_grad = jnp.sum(grads_rep.astype(jnp.float32) * returned, axis=1).reshape(
        tok_count, top_count
    )
    grads_back = lax.all_to_all(row_grad, ("node", "local"), split_axis=0, concat_axis=0, tiled=True)
    input_grad = lax.dot_general(
        picker.reshape(experts, cap_rows, tok_count),
        grads_back,
        (((0, 1), (0, 1)), ((), ())),
        preferred_element_type=jnp.float32,
    ).astype(jnp.bfloat16)
    return (mixed, input_grad, combine_grad)


def solution(mesh):
    in_specs = (
        P(("node", "local"), None),
        P(("node", "local"), None),
        P(("node", "local"), None),
        P(("node", "local"), None, None),
        P(("node", "local"), None, None),
        P(("node", "local"), None, None),
        P(("node", "local"), None),
    )
    out_specs = (P(("node", "local"), None), P(("node", "local"), None), P(("node", "local"), None))
    return jax.shard_map(shards, mesh=mesh, in_specs=in_specs, out_specs=out_specs, check_vma=False)
```

```python
import jax
import jax.numpy as jnp
from jax import lax
from jax.sharding import PartitionSpec as P


def to_experts(buffers, experts, cap_rows):
    width = buffers[0].shape[1]
    shaped = tuple((item.reshape(experts, cap_rows, width) for item in buffers))
    arrived = (
        lax.all_to_all(shaped[0], ("node", "local"), split_axis=0, concat_axis=0, tiled=True),
        lax.all_to_all(shaped[1], ("node", "local"), split_axis=0, concat_axis=0, tiled=True),
    )
    return tuple((item.reshape(experts * cap_rows, width) for item in arrived))


def to_tokens(buffer, experts, cap_rows):
    width = buffer.shape[1]
    shaped = buffer.reshape(experts, cap_rows, width)
    return lax.all_to_all(shaped, ("node", "local"), split_axis=0, concat_axis=0, tiled=True)


def shards(tokens, expert_ids, combine, w_gate, w_up, w_down, grad_out):
    tok_count = tokens.shape[0]
    top_count = expert_ids.shape[1]
    width = tokens.shape[1]
    experts = lax.axis_size("node") * lax.axis_size("local")
    cap_rows = max(2, 3 * tok_count * top_count // (2 * experts))
    pair_ids = expert_ids.reshape(-1)
    named = expert_ids.T[:, :, None] == jnp.arange(experts, dtype=jnp.int32)[None, None, :]
    present = jnp.any(named, axis=0)
    token_weight = jnp.sum(jnp.where(named, combine.T[:, :, None], 0.0), axis=0)
    before = jnp.cumsum(present.astype(jnp.int32), axis=0) - present.astype(jnp.int32)
    slot = jnp.take_along_axis(before, expert_ids, axis=1).reshape(-1)
    weights = combine.reshape(-1)
    grads_rep = jnp.repeat(grad_out, top_count, axis=0)
    chosen = present[:, :, None] & (before[:, :, None] == jnp.arange(cap_rows, dtype=jnp.int32))
    slot_weight = jnp.sum(jnp.where(chosen, token_weight[:, :, None], 0.0), axis=0).reshape(-1)
    picker = jnp.transpose(chosen, (1, 2, 0)).reshape(experts * cap_rows, tok_count)
    picker = picker.astype(jnp.bfloat16)
    send_rows = jnp.dot(picker, tokens, preferred_element_type=jnp.float32).astype(jnp.bfloat16)
    picked_grads = jnp.dot(picker, grad_out, preferred_element_type=jnp.float32)
    send_grads = (picked_grads * slot_weight[:, None]).astype(jnp.bfloat16)
    wg = w_gate[0]
    wu = w_up[0]
    wd = w_down[0]
    arrived, grads_in = to_experts((send_rows, send_grads), experts, cap_rows)
    gate = jnp.dot(arrived, wg, preferred_element_type=jnp.float32)
    upper = jnp.dot(arrived, wu, preferred_element_type=jnp.float32)
    sigma = jax.nn.sigmoid(gate)
    active = gate * sigma
    hidden = (active * upper).astype(jnp.bfloat16)
    expert_out = jnp.dot(hidden, wd, preferred_element_type=jnp.float32).astype(jnp.bfloat16)
    returned_all = to_tokens(expert_out, experts, cap_rows)
    hidden_grad = lax.dot_general(
        grads_in, wd, (((1,), (1,)), ((), ())), preferred_element_type=jnp.float32
    )
    gate_grad = (hidden_grad * upper * sigma * (1.0 + gate * (1.0 - sigma))).astype(jnp.bfloat16)
    up_grad = (hidden_grad * active).astype(jnp.bfloat16)
    row_grad = lax.dot_general(
        gate_grad, wg, (((1,), (1,)), ((), ())), preferred_element_type=jnp.float32
    )
    row_grad = row_grad + lax.dot_general(
        up_grad, wu, (((1,), (1,)), ((), ())), preferred_element_type=jnp.float32
    )
    row_grad = row_grad.astype(jnp.bfloat16)
    row_grad = row_grad.reshape(experts, cap_rows, width)
    returned_all, row_grad = lax.optimization_barrier((returned_all, row_grad))
    returned = returned_all[pair_ids, slot].astype(jnp.float32)
    mixed = jnp.sum(
        (returned * weights[:, None]).reshape(tok_count, top_count, width), axis=1
    ).astype(jnp.bfloat16)
    combine_grad = jnp.sum(grads_rep.astype(jnp.float32) * returned, axis=1).reshape(
        tok_count, top_count
    )
    grads_back = lax.all_to_all(row_grad, ("node", "local"), split_axis=0, concat_axis=0, tiled=True)
    input_grad = lax.dot_general(
        picker.reshape(experts, cap_rows, tok_count),
        grads_back,
        (((0, 1), (0, 1)), ((), ())),
        preferred_element_type=jnp.float32,
    ).astype(jnp.bfloat16)
    return (mixed, input_grad, combine_grad)


def solution(mesh):
    in_specs = (
        P(("node", "local"), None),
        P(("node", "local"), None),
        P(("node", "local"), None),
        P(("node", "local"), None, None),
        P(("node", "local"), None, None),
        P(("node", "local"), None, None),
        P(("node", "local"), None),
    )
    out_specs = (P(("node", "local"), None), P(("node", "local"), None), P(("node", "local"), None))
    return jax.shard_map(shards, mesh=mesh, in_specs=in_specs, out_specs=out_specs, check_vma=False)
```

```python
import jax
import jax.numpy as jnp
from jax import lax
from jax.sharding import PartitionSpec as P


def to_experts(buffers, experts, cap_rows):
    width = buffers[0].shape[1]
    shaped = tuple((item.reshape(experts, cap_rows, width) for item in buffers))
    arrived = (
        lax.all_to_all(shaped[0], ("node", "local"), split_axis=0, concat_axis=0, tiled=True),
        lax.all_to_all(shaped[1], ("node", "local"), split_axis=0, concat_axis=0, tiled=True),
    )
    return tuple((item.reshape(experts * cap_rows, width) for item in arrived))


def to_tokens(buffer, experts, cap_rows):
    width = buffer.shape[1]
    shaped = buffer.reshape(experts, cap_rows, width)
    return lax.all_to_all(shaped, ("node", "local"), split_axis=0, concat_axis=0, tiled=True)


def shards(tokens, expert_ids, combine, w_gate, w_up, w_down, grad_out):
    tok_count = tokens.shape[0]
    top_count = expert_ids.shape[1]
    width = tokens.shape[1]
    experts = lax.axis_size("node") * lax.axis_size("local")
    cap_rows = max(2, 3 * tok_count * top_count // (2 * experts))
    pair_ids = expert_ids.reshape(-1)
    named = expert_ids.T[:, :, None] == jnp.arange(experts, dtype=jnp.int32)[None, None, :]
    present = jnp.any(named, axis=0)
    token_weight = jnp.sum(jnp.where(named, combine.T[:, :, None], 0.0), axis=0)
    order = jnp.arange(tok_count, dtype=jnp.int32)
    earlier = (order[None, :] < order[:, None]).astype(jnp.bfloat16)
    before = jnp.dot(earlier, present.astype(jnp.bfloat16), preferred_element_type=jnp.float32)
    before = before.astype(jnp.int32)
    slot = jnp.take_along_axis(before, expert_ids, axis=1).reshape(-1)
    weights = combine.reshape(-1)
    grads_rep = jnp.repeat(grad_out, top_count, axis=0)
    chosen = present[:, :, None] & (before[:, :, None] == jnp.arange(cap_rows, dtype=jnp.int32))
    slot_weight = jnp.sum(jnp.where(chosen, token_weight[:, :, None], 0.0), axis=0).reshape(-1)
    picker = jnp.transpose(chosen, (1, 2, 0)).reshape(experts * cap_rows, tok_count)
    picker = picker.astype(jnp.bfloat16)
    send_rows = jnp.dot(picker, tokens, preferred_element_type=jnp.float32).astype(jnp.bfloat16)
    picked_grads = jnp.dot(picker, grad_out, preferred_element_type=jnp.float32)
    send_grads = (picked_grads * slot_weight[:, None]).astype(jnp.bfloat16)
    wg = w_gate[0]
    wu = w_up[0]
    wd = w_down[0]
    arrived, grads_in = to_experts((send_rows, send_grads), experts, cap_rows)
    gate = jnp.dot(arrived, wg, preferred_element_type=jnp.float32)
    upper = jnp.dot(arrived, wu, preferred_element_type=jnp.float32)
    sigma = jax.nn.sigmoid(gate)
    active = gate * sigma
    hidden = (active * upper).astype(jnp.bfloat16)
    expert_out = jnp.dot(hidden, wd, preferred_element_type=jnp.float32).astype(jnp.bfloat16)
    returned_all = to_tokens(expert_out, experts, cap_rows)
    hidden_grad = lax.dot_general(
        grads_in, wd, (((1,), (1,)), ((), ())), preferred_element_type=jnp.float32
    )
    gate_grad = (hidden_grad * upper * sigma * (1.0 + gate * (1.0 - sigma))).astype(jnp.bfloat16)
    up_grad = (hidden_grad * active).astype(jnp.bfloat16)
    row_grad = lax.dot_general(
        gate_grad, wg, (((1,), (1,)), ((), ())), preferred_element_type=jnp.float32
    )
    row_grad = row_grad + lax.dot_general(
        up_grad, wu, (((1,), (1,)), ((), ())), preferred_element_type=jnp.float32
    )
    row_grad = row_grad.astype(jnp.bfloat16)
    row_grad = row_grad.reshape(experts, cap_rows, width)
    returned_all, row_grad = lax.optimization_barrier((returned_all, row_grad))
    returned = returned_all[pair_ids, slot].astype(jnp.float32)
    mixed = jnp.sum(
        (returned * weights[:, None]).reshape(tok_count, top_count, width), axis=1
    ).astype(jnp.bfloat16)
    combine_grad = jnp.sum(grads_rep.astype(jnp.float32) * returned, axis=1).reshape(
        tok_count, top_count
    )
    grads_back = lax.all_to_all(row_grad, ("node", "local"), split_axis=0, concat_axis=0, tiled=True)
    input_grad = lax.dot_general(
        picker.reshape(experts, cap_rows, tok_count),
        grads_back,
        (((0, 1), (0, 1)), ((), ())),
        preferred_element_type=jnp.float32,
    ).astype(jnp.bfloat16)
    return (mixed, input_grad, combine_grad)


def solution(mesh):
    in_specs = (
        P(("node", "local"), None),
        P(("node", "local"), None),
        P(("node", "local"), None),
        P(("node", "local"), None, None),
        P(("node", "local"), None, None),
        P(("node", "local"), None, None),
        P(("node", "local"), None),
    )
    out_specs = (P(("node", "local"), None), P(("node", "local"), None), P(("node", "local"), None))
    return jax.shard_map(shards, mesh=mesh, in_specs=in_specs, out_specs=out_specs, check_vma=False)
```

```python
import jax
import jax.numpy as jnp
from jax import lax
from jax.sharding import PartitionSpec as P


def to_experts(buffers, experts, cap_rows):
    width = buffers[0].shape[1]
    shaped = tuple((item.reshape(experts, cap_rows, width) for item in buffers))
    arrived = (
        lax.all_to_all(shaped[0], ("local", "node"), split_axis=0, concat_axis=0, tiled=True),
        lax.all_to_all(shaped[1], ("local", "node"), split_axis=0, concat_axis=0, tiled=True),
    )
    return tuple((item.reshape(experts * cap_rows, width) for item in arrived))


def to_tokens(buffer, experts, cap_rows):
    width = buffer.shape[1]
    shaped = buffer.reshape(experts, cap_rows, width)
    return lax.all_to_all(shaped, ("local", "node"), split_axis=0, concat_axis=0, tiled=True)


def shards(tokens, expert_ids, combine, w_gate, w_up, w_down, grad_out):
    tok_count = tokens.shape[0]
    top_count = expert_ids.shape[1]
    width = tokens.shape[1]
    experts = lax.axis_size("node") * lax.axis_size("local")
    cap_rows = max(2, 3 * tok_count * top_count // (2 * experts))
    pair_ids = expert_ids.reshape(-1)
    named = expert_ids.T[:, :, None] == jnp.arange(experts, dtype=jnp.int32)[None, None, :]
    present = jnp.any(named, axis=0)
    token_weight = jnp.sum(jnp.where(named, combine.T[:, :, None], 0.0), axis=0)
    before = jnp.cumsum(present.astype(jnp.int32), axis=0) - present.astype(jnp.int32)
    slot = jnp.take_along_axis(before, expert_ids, axis=1).reshape(-1)
    weights = combine.reshape(-1)
    grads_rep = jnp.repeat(grad_out, top_count, axis=0)
    chosen = present[:, :, None] & (before[:, :, None] == jnp.arange(cap_rows, dtype=jnp.int32))
    nodes, locals_ = lax.axis_size("node"), lax.axis_size("local")
    chosen = chosen.reshape(tok_count, nodes, locals_, cap_rows).transpose(0, 2, 1, 3)
    chosen = chosen.reshape(tok_count, experts, cap_rows)
    token_weight = token_weight.reshape(tok_count, nodes, locals_).transpose(0, 2, 1)
    token_weight = token_weight.reshape(tok_count, experts)
    chunk_of_pair = (pair_ids % locals_) * nodes + pair_ids // locals_
    slot_weight = jnp.sum(jnp.where(chosen, token_weight[:, :, None], 0.0), axis=0).reshape(-1)
    picker = jnp.transpose(chosen, (1, 2, 0)).reshape(experts * cap_rows, tok_count)
    picker = picker.astype(jnp.bfloat16)
    send_rows = jnp.dot(picker, tokens, preferred_element_type=jnp.float32).astype(jnp.bfloat16)
    picked_grads = jnp.dot(picker, grad_out, preferred_element_type=jnp.float32)
    send_grads = (picked_grads * slot_weight[:, None]).astype(jnp.bfloat16)
    wg = w_gate[0]
    wu = w_up[0]
    wd = w_down[0]
    arrived, grads_in = to_experts((send_rows, send_grads), experts, cap_rows)
    gate = jnp.dot(arrived, wg, preferred_element_type=jnp.float32)
    upper = jnp.dot(arrived, wu, preferred_element_type=jnp.float32)
    sigma = jax.nn.sigmoid(gate)
    active = gate * sigma
    hidden = (active * upper).astype(jnp.bfloat16)
    expert_out = jnp.dot(hidden, wd, preferred_element_type=jnp.float32).astype(jnp.bfloat16)
    returned_all = to_tokens(expert_out, experts, cap_rows)
    hidden_grad = lax.dot_general(
        grads_in, wd, (((1,), (1,)), ((), ())), preferred_element_type=jnp.float32
    )
    gate_grad = (hidden_grad * upper * sigma * (1.0 + gate * (1.0 - sigma))).astype(jnp.bfloat16)
    up_grad = (hidden_grad * active).astype(jnp.bfloat16)
    row_grad = lax.dot_general(
        gate_grad, wg, (((1,), (1,)), ((), ())), preferred_element_type=jnp.float32
    )
    row_grad = row_grad + lax.dot_general(
        up_grad, wu, (((1,), (1,)), ((), ())), preferred_element_type=jnp.float32
    )
    row_grad = row_grad.astype(jnp.bfloat16)
    row_grad = row_grad.reshape(experts, cap_rows, width)
    returned_all, row_grad = lax.optimization_barrier((returned_all, row_grad))
    returned = returned_all[chunk_of_pair, slot].astype(jnp.float32)
    mixed = jnp.sum(
        (returned * weights[:, None]).reshape(tok_count, top_count, width), axis=1
    ).astype(jnp.bfloat16)
    combine_grad = jnp.sum(grads_rep.astype(jnp.float32) * returned, axis=1).reshape(
        tok_count, top_count
    )
    grads_back = lax.all_to_all(row_grad, ("local", "node"), split_axis=0, concat_axis=0, tiled=True)
    input_grad = lax.dot_general(
        picker.reshape(experts, cap_rows, tok_count),
        grads_back,
        (((0, 1), (0, 1)), ((), ())),
        preferred_element_type=jnp.float32,
    ).astype(jnp.bfloat16)
    return (mixed, input_grad, combine_grad)


def solution(mesh):
    in_specs = (
        P(("node", "local"), None),
        P(("node", "local"), None),
        P(("node", "local"), None),
        P(("node", "local"), None, None),
        P(("node", "local"), None, None),
        P(("node", "local"), None, None),
        P(("node", "local"), None),
    )
    out_specs = (P(("node", "local"), None), P(("node", "local"), None), P(("node", "local"), None))
    return jax.shard_map(shards, mesh=mesh, in_specs=in_specs, out_specs=out_specs, check_vma=False)
```

```python
import jax
import jax.numpy as jnp
from jax import lax
from jax.sharding import PartitionSpec as P


def to_experts(buffers, experts, cap_rows):
    width = buffers[0].shape[1]
    shaped = tuple((item.reshape(experts, cap_rows, width) for item in buffers))
    arrived = (
        lax.all_to_all(shaped[0], ("local", "node"), split_axis=0, concat_axis=0, tiled=True),
        lax.all_to_all(shaped[1], ("local", "node"), split_axis=0, concat_axis=0, tiled=True),
    )
    return tuple((item.reshape(experts * cap_rows, width) for item in arrived))


def to_tokens(buffer, experts, cap_rows):
    width = buffer.shape[1]
    shaped = buffer.reshape(experts, cap_rows, width)
    return lax.all_to_all(shaped, ("local", "node"), split_axis=0, concat_axis=0, tiled=True)


def shards(tokens, expert_ids, combine, w_gate, w_up, w_down, grad_out):
    tok_count = tokens.shape[0]
    top_count = expert_ids.shape[1]
    width = tokens.shape[1]
    experts = lax.axis_size("node") * lax.axis_size("local")
    cap_rows = max(2, 3 * tok_count * top_count // (2 * experts))
    pair_ids = expert_ids.reshape(-1)
    nodes, locals_ = lax.axis_size("node"), lax.axis_size("local")
    chunk = jnp.arange(experts, dtype=jnp.int32)
    expert_of_chunk = (chunk % nodes) * locals_ + chunk // nodes
    named = expert_ids.T[:, :, None] == expert_of_chunk[None, None, :]
    present = jnp.any(named, axis=0)
    token_weight = jnp.sum(jnp.where(named, combine.T[:, :, None], 0.0), axis=0)
    before = jnp.cumsum(present.astype(jnp.int32), axis=0) - present.astype(jnp.int32)
    chunk_ids = (expert_ids % locals_) * nodes + expert_ids // locals_
    slot = jnp.take_along_axis(before, chunk_ids, axis=1).reshape(-1)
    weights = combine.reshape(-1)
    grads_rep = jnp.repeat(grad_out, top_count, axis=0)
    chosen = present[:, :, None] & (before[:, :, None] == jnp.arange(cap_rows, dtype=jnp.int32))
    chunk_of_pair = chunk_ids.reshape(-1)
    slot_weight = jnp.sum(jnp.where(chosen, token_weight[:, :, None], 0.0), axis=0).reshape(-1)
    picker = jnp.transpose(chosen, (1, 2, 0)).reshape(experts * cap_rows, tok_count)
    picker = picker.astype(jnp.bfloat16)
    send_rows = jnp.dot(picker, tokens, preferred_element_type=jnp.float32).astype(jnp.bfloat16)
    picked_grads = jnp.dot(picker, grad_out, preferred_element_type=jnp.float32)
    send_grads = (picked_grads * slot_weight[:, None]).astype(jnp.bfloat16)
    wg = w_gate[0]
    wu = w_up[0]
    wd = w_down[0]
    arrived, grads_in = to_experts((send_rows, send_grads), experts, cap_rows)
    gate = jnp.dot(arrived, wg, preferred_element_type=jnp.float32)
    upper = jnp.dot(arrived, wu, preferred_element_type=jnp.float32)
    sigma = jax.nn.sigmoid(gate)
    active = gate * sigma
    hidden = (active * upper).astype(jnp.bfloat16)
    expert_out = jnp.dot(hidden, wd, preferred_element_type=jnp.float32).astype(jnp.bfloat16)
    returned_all = to_tokens(expert_out, experts, cap_rows)
    hidden_grad = lax.dot_general(
        grads_in, wd, (((1,), (1,)), ((), ())), preferred_element_type=jnp.float32
    )
    gate_grad = (hidden_grad * upper * sigma * (1.0 + gate * (1.0 - sigma))).astype(jnp.bfloat16)
    up_grad = (hidden_grad * active).astype(jnp.bfloat16)
    row_grad = lax.dot_general(
        gate_grad, wg, (((1,), (1,)), ((), ())), preferred_element_type=jnp.float32
    )
    row_grad = row_grad + lax.dot_general(
        up_grad, wu, (((1,), (1,)), ((), ())), preferred_element_type=jnp.float32
    )
    row_grad = row_grad.astype(jnp.bfloat16)
    row_grad = row_grad.reshape(experts, cap_rows, width)
    returned_all, row_grad = lax.optimization_barrier((returned_all, row_grad))
    returned = returned_all[chunk_of_pair, slot].astype(jnp.float32)
    mixed = jnp.sum(
        (returned * weights[:, None]).reshape(tok_count, top_count, width), axis=1
    ).astype(jnp.bfloat16)
    combine_grad = jnp.sum(grads_rep.astype(jnp.float32) * returned, axis=1).reshape(
        tok_count, top_count
    )
    grads_back = lax.all_to_all(row_grad, ("local", "node"), split_axis=0, concat_axis=0, tiled=True)
    input_grad = lax.dot_general(
        picker.reshape(experts, cap_rows, tok_count),
        grads_back,
        (((0, 1), (0, 1)), ((), ())),
        preferred_element_type=jnp.float32,
    ).astype(jnp.bfloat16)
    return (mixed, input_grad, combine_grad)


def solution(mesh):
    in_specs = (
        P(("node", "local"), None),
        P(("node", "local"), None),
        P(("node", "local"), None),
        P(("node", "local"), None, None),
        P(("node", "local"), None, None),
        P(("node", "local"), None, None),
        P(("node", "local"), None),
    )
    out_specs = (P(("node", "local"), None), P(("node", "local"), None), P(("node", "local"), None))
    return jax.shard_map(shards, mesh=mesh, in_specs=in_specs, out_specs=out_specs, check_vma=False)
```
